1024 devices in a mesh: seq: 32 (over y, z_lo), head: 32 (over x, z_hi, core).
Axes of the slice: x: 4, y: 4, z: 32 (z_hi: 4, z_lo: 8; z = z_hi * 8 + z_lo), core: 2. Of those that a mesh axis runs over, the one named last changes fastest.
Arguments:
- query_heads: bfloat16 [16384, 4096], P('seq', 'head'), may hold values from -5 to 5
- key_heads: bfloat16 [16384, 4096], P('seq', 'head'), may hold values from -5 to 5
- value_heads: bfloat16 [16384, 4096], P('seq', 'head'), may hold values from -6 to 6
- grad_out: bfloat16 [16384, 4096], P(('seq', 'head')), may hold values from -6 to 6
- saved_out: bfloat16 [16384, 4096], P(('seq', 'head')), may hold values from -6 to 6
- block_list: int32 [128, 8], replicated, may hold values from -1 to 7, as said below
Outputs:
- grad_query: bfloat16 [16384, 4096], P(('seq', 'head'))
- grad_key: bfloat16 [16384, 4096], P(('seq', 'head'))
- grad_value: bfloat16 [16384, 4096], P(('seq', 'head'))
The draws below stay inside these ranges and needn't reach their ends.
Inputs may be any that keep to these rules, and one draw needn't show every extreme that they name: `block_list`: row b lists first its own diagonal block 4 + b % 4, then distinct earlier blocks of its own group or blocks of the preceding group (none for the first group), then -1 for the remaining entries; the last query block of the sequence lists 8 blocks.
All inputs are finite; a program needn't handle non-finite values.
Results may differ from the reference program's by a relative error of at most 0.0065.
Values may be sent and summed in bfloat16 or wider, within the bound.
No kernel may reach another device: no remote copies, remote signals or barrier semaphores. Data moves between devices by JAX's collectives and lax.ppermute only.
A program may use at most 32 MiB of HBM per device.

```python
from functools import partial
import jax
import jax.numpy as jnp
from jax import lax

HD = 128
BLK = 128
MAXSEL = 8
QB = 4
HEADS = 32
D = 4096
TOKENS = 16384
QB_ALL = 128
N_SEQ = 32


def query_key_pair(key):
    base_key = jax.random.fold_in(key, 7001)
    queries = jax.random.normal(jax.random.fold_in(base_key, 1), (TOKENS, D), jnp.float32)
    key_rows = jax.random.normal(jax.random.fold_in(base_key, 2), (TOKENS, D), jnp.float32)
    return (jnp.clip(queries, -5.0, 5.0), jnp.clip(key_rows, -5.0, 5.0))


def draw_query_heads(key, part):
    return query_key_pair(key)[0].astype(jnp.bfloat16)


def draw_key_heads(key, part):
    return query_key_pair(key)[1].astype(jnp.bfloat16)


def draw_block_list(key, part):
    base_key = jax.random.fold_in(key, 9103)
    row_ids = jnp.arange(QB_ALL, dtype=jnp.int32)
    group_ids = row_ids // QB
    block_ids = row_ids % QB
    col_ids = jnp.arange(2 * QB, dtype=jnp.int32)
    available = (col_ids[None, :] < QB) & (group_ids[:, None] > 0) | (col_ids[None, :] >= QB) & (col_ids[None, :] < QB + block_ids[:, None])
    count_available = jnp.sum(available.astype(jnp.int32), axis=1)
    wanted = jax.random.randint(jax.random.fold_in(base_key, 1), (QB_ALL,), 0, MAXSEL, jnp.int32)
    wanted = jnp.where(row_ids == QB_ALL - 1, MAXSEL - 1, wanted)
    extra_count = jnp.minimum(wanted, count_available)
    rank_score = jax.random.randint(jax.random.fold_in(base_key, 2), (QB_ALL, 2 * QB), 0, 2 ** 20, jnp.int32) * (2 * QB) + col_ids[None, :]
    rank_score = jnp.where(available, rank_score, -1)
    best_scores, _ = lax.top_k(rank_score, MAXSEL - 1)
    picked = best_scores % (2 * QB)
    slot_ids = jnp.arange(MAXSEL - 1, dtype=jnp.int32)
    picked = jnp.where(slot_ids[None, :] < extra_count[:, None], picked, -1)
    return jnp.concatenate([(QB + block_ids)[:, None], picked], axis=1).astype(jnp.int32)


def steps_of(own_key, dims, shards, smallest, high):
    loudness = 1.0
    for position, blocks in shards:
        heights = jax.random.uniform(jax.random.fold_in(jax.random.fold_in(own_key, 6), position), (blocks,), jnp.float32, smallest / len(shards), high / len(shards))
        loudness = loudness * jnp.repeat(jnp.exp(heights), dims[position] // blocks).reshape((-1,) + (1,) * (len(dims) - 1 - position))
    return loudness


def noise(key, extent, width, limit, shards=(), held_as=jnp.bfloat16):
    factor_of = steps_of(key, extent, shards, -0.22, 0.18) if shards else 1.0
    drawn = jax.random.normal(key, extent, jnp.float32) * width * factor_of
    return jnp.minimum(jnp.maximum(drawn, -limit), limit).astype(held_as)


def setup_inputs(seed: int = 0) -> dict:
    keys = jax.random.split(jax.random.key(seed), 7)
    return {
        "query_heads": draw_query_heads(jax.random.fold_in(keys[6], 71), 0),
        "key_heads": draw_key_heads(jax.random.fold_in(keys[6], 71), 0),
        "value_heads": noise(keys[2], (TOKENS, D), 1.0, 6.0, ((0, 32), (1, 32))),
        "grad_out": noise(keys[3], (TOKENS, D), 1.0, 6.0, ((0, 1024),)),
        "saved_out": noise(keys[4], (TOKENS, D), 1.0, 6.0, ((0, 1024),)),
        "block_list": draw_block_list(jax.random.fold_in(keys[6], 71), 0),
    }


def block_scores(query_blocks, key_blocks, block_index, key_limit):
    qcount = query_blocks.shape[0]
    picked = jnp.maximum(block_index, 0)
    key_tiles = key_blocks[picked]
    scores = jnp.einsum("qid,qjd->qij", query_blocks.astype(jnp.float32), key_tiles.astype(jnp.float32)) * (HD ** -0.5)
    diagonal = block_index == (qcount + jnp.arange(qcount, dtype=jnp.int32))
    lower_mask = jnp.arange(BLK, dtype=jnp.int32)[:, None] >= jnp.arange(BLK, dtype=jnp.int32)[None, :]
    allowed = ((block_index >= 0) & (block_index < key_limit))[:, None, None] & ((~diagonal)[:, None, None] | lower_mask[None])
    return picked, key_tiles, scores, allowed


def log_totals(query_blocks, key_blocks, block_rows):
    qcount = query_blocks.shape[0]
    running_max = jnp.full((qcount, BLK), -1e30, jnp.float32)
    running_sum = jnp.zeros((qcount, BLK), jnp.float32)
    for slot_index in range(MAXSEL):
        _, _, scores, allowed = block_scores(query_blocks, key_blocks, block_rows[:, slot_index], 2 * qcount)
        masked = jnp.where(allowed, scores, -1e30)
        new_max = jnp.maximum(running_max, jnp.max(masked, axis=2))
        running_sum = running_sum * jnp.exp(running_max - new_max) + jnp.sum(jnp.where(allowed, jnp.exp(masked - new_max[:, :, None]), 0.0), axis=2)
        running_max = new_max
    return running_max + jnp.log(running_sum)


def tile_grads(query_blocks, grad_blocks, log_norm, row_delta, key_blocks, value_blocks, block_rows, key_limit):
    qcount = query_blocks.shape[0]
    grad_query = jnp.zeros((qcount, BLK, HD), jnp.float32)
    grad_keys = jnp.zeros(key_blocks.shape, jnp.float32)
    grad_values = jnp.zeros(key_blocks.shape, jnp.float32)
    for slot_index in range(MAXSEL):
        picked, key_tiles, scores, allowed = block_scores(query_blocks, key_blocks, block_rows[:, slot_index], key_limit)
        probabilities = jnp.exp(jnp.where(allowed, scores - log_norm[:, :, None], -1e30))
        value_tiles = value_blocks[picked]
        prob_grad = jnp.einsum("qid,qjd->qij", grad_blocks.astype(jnp.float32), value_tiles.astype(jnp.float32))
        score_grad = (probabilities * (prob_grad - row_delta[:, :, None])).astype(jnp.bfloat16)
        prob_round = probabilities.astype(jnp.bfloat16)
        grad_query = grad_query + jnp.einsum("qij,qjd->qid", score_grad.astype(jnp.float32), key_tiles.astype(jnp.float32)) * (HD ** -0.5)
        grad_keys = grad_keys.at[picked].add(jnp.einsum("qij,qid->qjd", score_grad.astype(jnp.float32), query_blocks.astype(jnp.float32)) * (HD ** -0.5))
        grad_values = grad_values.at[picked].add(jnp.einsum("qij,qid->qjd", prob_round.astype(jnp.float32), grad_blocks.astype(jnp.float32)))
    return grad_query, grad_keys, grad_values


def group_grads(query_blocks, key_blocks, value_blocks, grad_blocks, saved_blocks, block_rows):
    row_delta = jnp.sum(grad_blocks.astype(jnp.float32) * saved_blocks.astype(jnp.float32), axis=-1)
    log_norm = log_totals(query_blocks, key_blocks, block_rows)
    return tile_grads(query_blocks, grad_blocks, log_norm, row_delta, key_blocks, value_blocks, block_rows, 2 * QB)


def head_grads(head_items, block_rows):
    query_part, key_part, value_part, grad_part, saved_part = head_items
    empty_rows = jnp.zeros_like(key_part[:1])
    key_blocks = jnp.concatenate([jnp.concatenate([empty_rows, key_part[:-1]], axis=0), key_part], axis=1)
    value_blocks = jnp.concatenate([jnp.concatenate([empty_rows, value_part[:-1]], axis=0), value_part], axis=1)
    grad_query, grad_keys, grad_values = jax.vmap(group_grads)(query_part, key_blocks, value_blocks, grad_part, saved_part, block_rows)
    empty_grad = jnp.zeros_like(grad_keys[:1, :QB])
    own_keys = grad_keys[:, QB:] + jnp.concatenate([grad_keys[1:, :QB], empty_grad], axis=0)
    own_values = grad_values[:, QB:] + jnp.concatenate([grad_values[1:, :QB], empty_grad], axis=0)
    return grad_query.astype(jnp.bfloat16), own_keys.astype(jnp.bfloat16), own_values.astype(jnp.bfloat16)


def heads_first(matrix):
    return matrix.reshape(N_SEQ, QB, BLK, HEADS, HD).transpose(3, 0, 1, 2, 4)


def tokens_first(matrix):
    return matrix.transpose(1, 2, 3, 0, 4).reshape(TOKENS, D)


def reference(query_heads, key_heads, value_heads, grad_out, saved_out, block_list):
    block_rows = block_list.reshape(N_SEQ, QB, MAXSEL)
    stacked = (heads_first(query_heads), heads_first(key_heads), heads_first(value_heads), heads_first(grad_out), heads_first(saved_out))
    grad_query, grad_key, grad_value = lax.map(partial(head_grads, block_rows=block_rows), stacked)
    return tokens_first(grad_query), tokens_first(grad_key), tokens_first(grad_value)
```

```python
import functools

import jax
import jax.numpy as jnp
from jax import lax
from jax.experimental import pallas as pl
from jax.experimental.pallas import tpu as pltpu
from jax.sharding import PartitionSpec as P

HD = 128
BLK = 128
MAXSEL = 8
SCALE = HD ** (-0.5)
MASKED = -1e30
LIMIT = 24 * 1024 * 1024
VM = pl.BlockSpec(memory_space=pltpu.VMEM)
SM = pl.BlockSpec(memory_space=pltpu.SMEM)
F32 = jnp.float32
BF16 = jnp.bfloat16


def shifted(value, axis, by):
    size = lax.axis_size(axis)
    pairs = [(i, i + by) for i in range(size) if 0 <= i + by < size]
    return lax.ppermute(value, axis, pairs)


def nt(a, b):
    return lax.dot_general(a, b, (((1,), (1,)), ((), ())), preferred_element_type=F32)


def nn(a, b):
    return lax.dot_general(a, b, (((1,), (0,)), ((), ())), preferred_element_type=F32)


def tn(a, b):
    return lax.dot_general(a, b, (((0,), (0,)), ((), ())), preferred_element_type=F32)


def call(body, ins, outs, name, flops, nbytes, scratch=()):
    return pl.pallas_call(
        body,
        in_specs=ins,
        out_specs=tuple(VM for _ in outs),
        out_shape=tuple(jax.ShapeDtypeStruct(s, d) for s, d in outs),
        scratch_shapes=list(scratch),
        compiler_params=pltpu.CompilerParams(vmem_limit_bytes=LIMIT),
        cost_estimate=pl.CostEstimate(flops=flops, bytes_accessed=nbytes, transcendentals=0),
        name=name,
    )


def pack_kernel(slot_ref, grad_ref, saved_ref, out_ref, square):
    heads, rows = out_ref.shape[0], grad_ref.shape[0]
    lane = lax.broadcasted_iota(jnp.int32, (rows, BLK), 1)
    delta = jnp.zeros((rows, BLK), F32)
    for h in range(heads):
        g = grad_ref[:, h * HD : (h + 1) * HD]
        out_ref[h, 0:rows, :] = g
        prod = g.astype(F32) * saved_ref[:, h * HD : (h + 1) * HD].astype(F32)
        delta = jnp.where(lane == h, jnp.sum(prod, axis=1, keepdims=True), delta)
    square[...] = jnp.zeros_like(square)
    start = pl.multiple_of(slot_ref[0] * rows, rows)
    square[pl.ds(start, rows), :] = delta
    turned = square[...].T
    high = turned.astype(BF16).astype(F32)
    rest = turned - high
    mid = rest.astype(BF16).astype(F32)
    low = rest - mid
    row = lax.broadcasted_iota(jnp.int32, (8, BLK), 0)
    for h in range(heads):
        parts = jnp.where(row == 0, high[h : h + 1, :], 0.0)
        parts = jnp.where(row == 1, mid[h : h + 1, :], parts)
        parts = jnp.where(row == 2, low[h : h + 1, :], parts)
        out_ref[h, rows : rows + 8, :] = parts.astype(BF16)


def prob_kernel(list_ref, q_ref, k_ref, prev_ref, p_ref):
    span = q_ref.shape[0]
    qcount = span // BLK
    listed = []
    for b in range(qcount):
        bits = jnp.int32(0)
        for slot in range(MAXSEL):
            entry = list_ref[b, slot]
            bits = bits | jnp.where(entry >= 0, jnp.int32(1) << jnp.maximum(entry, 0), 0)
        listed.append(bits)
    lane = lax.broadcasted_iota(jnp.int32, (1, 2 * BLK), 1)
    key_row = lax.broadcasted_iota(jnp.int32, (BLK, 2 * BLK), 0)
    query_col = lax.broadcasted_iota(jnp.int32, (BLK, 2 * BLK), 1)
    for pair in range(qcount // 2):
        first = 2 * pair
        cols = slice(first * BLK, (first + 2) * BLK)
        queries = q_ref[cols, :]
        bits = jnp.where(lane < BLK, listed[first], listed[first + 1])
        keys_of = [(j, prev_ref[j * BLK : (j + 1) * BLK, :]) for j in range(qcount)]
        keys_of += [
            (qcount + j, k_ref[j * BLK : (j + 1) * BLK, :]) for j in range(first + 2)
        ]
        top = jnp.full((BLK, 2 * BLK), MASKED, F32)
        for j, keys in keys_of:
            scores = nt(keys, queries) * SCALE
            allowed = jnp.broadcast_to(((bits >> j) & 1) == 1, scores.shape)
            if j >= qcount + first:
                own = (j - qcount - first) * BLK
                inside = (query_col >= own) & (query_col < own + BLK)
                allowed = allowed & (jnp.logical_not(inside) | (key_row <= query_col - own))
            scores = jnp.where(allowed, scores, MASKED)
            p_ref[j * BLK : (j + 1) * BLK, cols] = scores
            top = jnp.maximum(top, scores)
        top = jnp.max(top, axis=0, keepdims=True)
        total = jnp.zeros((BLK, 2 * BLK), F32)
        for j, _ in keys_of:
            e = jnp.exp(p_ref[j * BLK : (j + 1) * BLK, cols] - top)
            p_ref[j * BLK : (j + 1) * BLK, cols] = e
            total = total + e
        inverse = 1.0 / jnp.sum(total, axis=0, keepdims=True)
        for j, _ in keys_of:
            p_ref[j * BLK : (j + 1) * BLK, cols] = p_ref[j * BLK : (j + 1) * BLK, cols] * inverse
        for j in range(first + 2, qcount):
            rows = slice((qcount + j) * BLK, (qcount + j + 1) * BLK)
            p_ref[rows, cols] = jnp.zeros((BLK, 2 * BLK), F32)


def received(recv_ref):
    peers, slab = recv_ref.shape[0], recv_ref.shape[1]
    rows = slab - 8
    grads = recv_ref[:, 0:rows, :].reshape(peers * rows, HD)
    parts = recv_ref[:, rows:slab, :].astype(F32)
    each = BLK // rows
    deltas = [
        jnp.sum(jnp.sum(parts[b * each : (b + 1) * each], axis=0), axis=0, keepdims=True)
        for b in range(peers // each)
    ]
    return grads, deltas


def prev_kernel(p_ref, recv_ref, q_ref, prev_ref, back_ref, dq_ref):
    span = q_ref.shape[0]
    grads, deltas = received(recv_ref)
    delta = jnp.concatenate(deltas, axis=1)
    keys, values = prev_ref[0:span, :], prev_ref[span : 2 * span, :]
    p = p_ref[0:span, :]
    score_grad = (p * (nt(values, grads) - delta)).astype(BF16)
    back_ref[0:span, :] = (nn(score_grad, q_ref[...]) * SCALE).astype(BF16)
    back_ref[span : 2 * span, :] = nn(p.astype(BF16), grads).astype(BF16)
    dq_ref[...] = tn(score_grad, keys)


def own_kernel(p_ref, recv_ref, q_ref, k_ref, v_ref, part_ref, dq_ref, dkv_ref):
    span = q_ref.shape[0]
    grads, deltas = received(recv_ref)
    delta = jnp.concatenate(deltas, axis=1)
    p = p_ref[span : 2 * span, :]
    score_grad = (p * (nt(v_ref[...], grads) - delta)).astype(BF16)
    dkv_ref[0:span, :] = nn(score_grad, q_ref[...]) * SCALE
    dkv_ref[span : 2 * span, :] = nn(p.astype(BF16), grads)
    dq_ref[...] = ((part_ref[...] + tn(score_grad, k_ref[...])) * SCALE).astype(BF16)


def join_kernel(dq_ref, dkv_ref, back_ref, out_ref):
    peers, rows = out_ref.shape[0], out_ref.shape[1] // 3
    span = dq_ref.shape[0]
    out_ref[:, 0:rows, :] = dq_ref[...].reshape(peers, rows, HD)
    both = (dkv_ref[...] + back_ref[...].astype(F32)).astype(BF16)
    out_ref[:, rows : 2 * rows, :] = both[0:span].reshape(peers, rows, HD)
    out_ref[:, 2 * rows : 3 * rows, :] = both[span:].reshape(peers, rows, HD)


def split_kernel(in_ref, dq_ref, dk_ref, dv_ref):
    peers, rows = in_ref.shape[0], in_ref.shape[1] // 3
    for h in range(peers):
        for i, ref in enumerate((dq_ref, dk_ref, dv_ref)):
            ref[:, h * HD : (h + 1) * HD] = in_ref[h, i * rows : (i + 1) * rows, :]


def shards(query_heads, key_heads, value_heads, grad_out, saved_out, block_list):
    span = query_heads.shape[0]
    qcount = span // BLK
    heads = lax.axis_size("head")
    rows = grad_out.shape[0]
    slot = lax.rem(lax.axis_index("head"), BLK // rows).astype(jnp.int32)[None]
    (packed,) = call(
        pack_kernel,
        [SM, VM, VM],
        [((heads, rows + 8, HD), BF16)],
        "pack",
        4 * rows * heads * HD,
        6 * rows * heads * HD,
        [pltpu.VMEM((BLK, BLK), F32)],
    )(slot, grad_out, saved_out)
    arrived = lax.all_to_all(packed, "head", split_axis=0, concat_axis=0, tiled=True)
    previous = shifted(jnp.concatenate([key_heads, value_heads], axis=0), "seq", 1)
    group_index = lax.axis_index("seq")
    block_rows = lax.dynamic_slice_in_dim(block_list, group_index * qcount, qcount, 0)
    (probs,) = call(
        prob_kernel,
        [SM, VM, VM, VM],
        [((2 * span, span), F32)],
        "probs",
        4 * span * span * HD,
        12 * span * span,
    )(block_rows, query_heads, key_heads, previous)
    back, dq_part = call(
        prev_kernel,
        [VM] * 4,
        [((2 * span, HD), BF16), ((span, HD), F32)],
        "prev_grads",
        8 * span * span * HD,
        8 * span * span,
    )(probs, arrived, query_heads, previous)
    returned = shifted(back, "seq", -1)
    grad_query, own = call(
        own_kernel,
        [VM] * 6,
        [((span, HD), BF16), ((2 * span, HD), F32)],
        "own_grads",
        8 * span * span * HD,
        8 * span * span,
    )(probs, arrived, query_heads, key_heads, value_heads, dq_part)
    (joined,) = call(
        join_kernel,
        [VM] * 3,
        [((heads, 3 * rows, HD), BF16)],
        "join",
        4 * span * HD,
        16 * span * HD,
    )(grad_query, own, returned)
    landed = lax.all_to_all(joined, "head", split_axis=0, concat_axis=0, tiled=True)
    return call(
        split_kernel,
        [VM],
        [((rows, heads * HD), BF16)] * 3,
        "split",
        0,
        12 * rows * heads * HD,
    )(landed)


def solution(mesh):
    placed = (
        P("seq", "head"),
        P("seq", "head"),
        P("seq", "head"),
        P(("seq", "head"), None),
        P(("seq", "head"), None),
        P(),
    )
    return jax.shard_map(
        shards,
        mesh=mesh,
        in_specs=placed,
        out_specs=(P(("seq", "head"), None), P(("seq", "head"), None), P(("seq", "head"), None)),
        check_vma=False,
    )
```

```python
import functools

import jax
import jax.numpy as jnp
from jax import lax
from jax.experimental import pallas as pl
from jax.experimental.pallas import tpu as pltpu
from jax.sharding import PartitionSpec as P

HD = 128
BLK = 128
MAXSEL = 8
SCALE = HD ** (-0.5)
MASKED = -1e30
LIMIT = 24 * 1024 * 1024
VM = pl.BlockSpec(memory_space=pltpu.VMEM)
SM = pl.BlockSpec(memory_space=pltpu.SMEM)
F32 = jnp.float32
BF16 = jnp.bfloat16


def shifted(value, axis, by):
    size = lax.axis_size(axis)
    pairs = [(i, i + by) for i in range(size) if 0 <= i + by < size]
    return lax.ppermute(value, axis, pairs)


def nt(a, b):
    return lax.dot_general(a, b, (((1,), (1,)), ((), ())), preferred_element_type=F32)


def nn(a, b):
    return lax.dot_general(a, b, (((1,), (0,)), ((), ())), preferred_element_type=F32)


def tn(a, b):
    return lax.dot_general(a, b, (((0,), (0,)), ((), ())), preferred_element_type=F32)


def call(body, ins, outs, name, flops, nbytes, scratch=()):
    return pl.pallas_call(
        body,
        in_specs=ins,
        out_specs=tuple(VM for _ in outs),
        out_shape=tuple(jax.ShapeDtypeStruct(s, d) for s, d in outs),
        scratch_shapes=list(scratch),
        compiler_params=pltpu.CompilerParams(vmem_limit_bytes=LIMIT),
        cost_estimate=pl.CostEstimate(flops=flops, bytes_accessed=nbytes, transcendentals=0),
        name=name,
    )


def pack_kernel(slot_ref, grad_ref, saved_ref, out_ref, square):
    heads, rows = out_ref.shape[0], grad_ref.shape[0]
    lane = lax.broadcasted_iota(jnp.int32, (rows, BLK), 1)
    delta = jnp.zeros((rows, BLK), F32)
    for h in range(heads):
        g = grad_ref[:, h * HD : (h + 1) * HD]
        for k in range(rows // 2):
            out_ref[h, k] = g[2 * k : 2 * k + 2, :]
        prod = g.astype(F32) * saved_ref[:, h * HD : (h + 1) * HD].astype(F32)
        delta = jnp.where(lane == h, jnp.sum(prod, axis=1, keepdims=True), delta)
    square[...] = jnp.zeros_like(square)
    start = pl.multiple_of(slot_ref[0] * rows, rows)
    square[pl.ds(start, rows), :] = delta
    turned = square[...].T
    high = turned.astype(BF16).astype(F32)
    rest = turned - high
    row = lax.broadcasted_iota(jnp.int32, (2, BLK), 0)
    for h in range(heads):
        parts = jnp.where(row == 0, high[h : h + 1, :], rest[h : h + 1, :])
        out_ref[h, rows // 2] = parts.astype(BF16)


def prob_kernel(list_ref, q_ref, k_ref, prev_ref, p_ref):
    span = q_ref.shape[0]
    qcount = span // BLK
    listed = []
    for b in range(qcount):
        bits = jnp.int32(0)
        for slot in range(MAXSEL):
            entry = list_ref[b, slot]
            bits = bits | jnp.where(entry >= 0, jnp.int32(1) << jnp.maximum(entry, 0), 0)
        listed.append(bits)
    lane = lax.broadcasted_iota(jnp.int32, (1, 2 * BLK), 1)
    key_row = lax.broadcasted_iota(jnp.int32, (BLK, 2 * BLK), 0)
    query_col = lax.broadcasted_iota(jnp.int32, (BLK, 2 * BLK), 1)
    for pair in range(qcount // 2):
        first = 2 * pair
        cols = slice(first * BLK, (first + 2) * BLK)
        queries = q_ref[cols, :]
        bits = jnp.where(lane < BLK, listed[first], listed[first + 1])
        keys_of = [(j, prev_ref[j * BLK : (j + 1) * BLK, :]) for j in range(qcount)]
        keys_of += [
            (qcount + j, k_ref[j * BLK : (j + 1) * BLK, :]) for j in range(first + 2)
        ]
        top = jnp.full((BLK, 2 * BLK), MASKED, F32)
        for j, keys in keys_of:
            scores = nt(keys, queries) * SCALE
            allowed = jnp.broadcast_to(((bits >> j) & 1) == 1, scores.shape)
            if j >= qcount + first:
                own = (j - qcount - first) * BLK
                inside = (query_col >= own) & (query_col < own + BLK)
                allowed = allowed & (jnp.logical_not(inside) | (key_row <= query_col - own))
            scores = jnp.where(allowed, scores, MASKED)
            p_ref[j * BLK : (j + 1) * BLK, cols] = scores
            top = jnp.maximum(top, scores)
        top = jnp.max(top, axis=0, keepdims=True)
        total = jnp.zeros((BLK, 2 * BLK), F32)
        for j, _ in keys_of:
            e = jnp.exp(p_ref[j * BLK : (j + 1) * BLK, cols] - top)
            p_ref[j * BLK : (j + 1) * BLK, cols] = e
            total = total + e
        inverse = 1.0 / jnp.sum(total, axis=0, keepdims=True)
        for j, _ in keys_of:
            p_ref[j * BLK : (j + 1) * BLK, cols] = p_ref[j * BLK : (j + 1) * BLK, cols] * inverse
        for j in range(first + 2, qcount):
            rows = slice((qcount + j) * BLK, (qcount + j + 1) * BLK)
            p_ref[rows, cols] = jnp.zeros((BLK, 2 * BLK), F32)


def received(recv_ref):
    peers, pairs = recv_ref.shape[0], recv_ref.shape[1] - 1
    rows = 2 * pairs
    grads = recv_ref[:, 0:pairs].reshape(peers * rows, HD)
    parts = jnp.sum(recv_ref[:, pairs].astype(F32), axis=1)
    each = BLK // rows
    deltas = [
        jnp.sum(parts[b * each : (b + 1) * each], axis=0, keepdims=True)
        for b in range(peers // each)
    ]
    return grads, deltas


def prev_kernel(p_ref, recv_ref, q_ref, prev_ref, back_ref, dq_ref):
    span = q_ref.shape[0]
    grads, deltas = received(recv_ref)
    delta = jnp.concatenate(deltas, axis=1)
    keys, values = prev_ref[0:span, :], prev_ref[span : 2 * span, :]
    p = p_ref[0:span, :]
    score_grad = (p * (nt(values, grads) - delta)).astype(BF16)
    back_ref[0:span, :] = (nn(score_grad, q_ref[...]) * SCALE).astype(BF16)
    back_ref[span : 2 * span, :] = nn(p.astype(BF16), grads).astype(BF16)
    dq_ref[...] = tn(score_grad, keys)


def own_kernel(p_ref, recv_ref, q_ref, k_ref, v_ref, part_ref, dq_ref, dkv_ref):
    span = q_ref.shape[0]
    grads, deltas = received(recv_ref)
    delta = jnp.concatenate(deltas, axis=1)
    p = p_ref[span : 2 * span, :]
    score_grad = (p * (nt(v_ref[...], grads) - delta)).astype(BF16)
    dkv_ref[0:span, :] = nn(score_grad, q_ref[...]) * SCALE
    dkv_ref[span : 2 * span, :] = nn(p.astype(BF16), grads)
    dq_ref[...] = ((part_ref[...] + tn(score_grad, k_ref[...])) * SCALE).astype(BF16)


def join_kernel(dq_ref, dkv_ref, back_ref, out_ref):
    peers, rows = out_ref.shape[0], out_ref.shape[1] // 3
    span = dq_ref.shape[0]
    out_ref[:, 0:rows, :] = dq_ref[...].reshape(peers, rows, HD)
    both = (dkv_ref[...] + back_ref[...].astype(F32)).astype(BF16)
    out_ref[:, rows : 2 * rows, :] = both[0:span].reshape(peers, rows, HD)
    out_ref[:, 2 * rows : 3 * rows, :] = both[span:].reshape(peers, rows, HD)


def split_kernel(in_ref, dq_ref, dk_ref, dv_ref):
    peers, rows = in_ref.shape[0], in_ref.shape[1] // 3
    for h in range(peers):
        for i, ref in enumerate((dq_ref, dk_ref, dv_ref)):
            ref[:, h * HD : (h + 1) * HD] = in_ref[h, i * rows : (i + 1) * rows, :]


def shards(query_heads, key_heads, value_heads, grad_out, saved_out, block_list):
    span = query_heads.shape[0]
    qcount = span // BLK
    heads = lax.axis_size("head")
    rows = grad_out.shape[0]
    slot = lax.rem(lax.axis_index("head"), BLK // rows).astype(jnp.int32)[None]
    (packed,) = call(
        pack_kernel,
        [SM, VM, VM],
        [((heads, rows // 2 + 1, 2, HD), BF16)],
        "pack",
        4 * rows * heads * HD,
        6 * rows * heads * HD,
        [pltpu.VMEM((BLK, BLK), F32)],
    )(slot, grad_out, saved_out)
    arrived = lax.all_to_all(packed, "head", split_axis=0, concat_axis=0, tiled=True)
    previous = shifted(jnp.concatenate([key_heads, value_heads], axis=0), "seq", 1)
    group_index = lax.axis_index("seq")
    block_rows = lax.dynamic_slice_in_dim(block_list, group_index * qcount, qcount, 0)
    (probs,) = call(
        prob_kernel,
        [SM, VM, VM, VM],
        [((2 * span, span), F32)],
        "probs",
        4 * span * span * HD,
        12 * span * span,
    )(block_rows, query_heads, key_heads, previous)
    back, dq_part = call(
        prev_kernel,
        [VM] * 4,
        [((2 * span, HD), BF16), ((span, HD), F32)],
        "prev_grads",
        8 * span * span * HD,
        8 * span * span,
    )(probs, arrived, query_heads, previous)
    returned = shifted(back, "seq", -1)
    grad_query, own = call(
        own_kernel,
        [VM] * 6,
        [((span, HD), BF16), ((2 * span, HD), F32)],
        "own_grads",
        8 * span * span * HD,
        8 * span * span,
    )(probs, arrived, query_heads, key_heads, value_heads, dq_part)
    (joined,) = call(
        join_kernel,
        [VM] * 3,
        [((heads, 3 * rows, HD), BF16)],
        "join",
        4 * span * HD,
        16 * span * HD,
    )(grad_query, own, returned)
    landed = lax.all_to_all(joined, "head", split_axis=0, concat_axis=0, tiled=True)
    return call(
        split_kernel,
        [VM],
        [((rows, heads * HD), BF16)] * 3,
        "split",
        0,
        12 * rows * heads * HD,
    )(landed)


def solution(mesh):
    placed = (
        P("seq", "head"),
        P("seq", "head"),
        P("seq", "head"),
        P(("seq", "head"), None),
        P(("seq", "head"), None),
        P(),
    )
    return jax.shard_map(
        shards,
        mesh=mesh,
        in_specs=placed,
        out_specs=(P(("seq", "head"), None), P(("seq", "head"), None), P(("seq", "head"), None)),
        check_vma=False,
    )
```

```python
import jax
import jax.numpy as jnp
from jax import lax
from jax.experimental import pallas as pl
from jax.experimental.pallas import tpu as pltpu
from jax.sharding import PartitionSpec as P


HD = 128
BLK = 128
MAXSEL = 8
SCALE = HD ** (-0.5)
MASKED = -1e30
LIMIT = 24 * 1024 * 1024
VM = pl.BlockSpec(memory_space=pltpu.VMEM)
SM = pl.BlockSpec(memory_space=pltpu.SMEM)
HB = pl.BlockSpec(memory_space=pltpu.HBM)
F32 = jnp.float32
BF16 = jnp.bfloat16


def shifted(value, axis, by):
    size = lax.axis_size(axis)
    pairs = [(i, i + by) for i in range(size) if 0 <= i + by < size]
    return lax.ppermute(value, axis, pairs)


def nt(a, b):
    return lax.dot_general(a, b, (((1,), (1,)), ((), ())), preferred_element_type=F32)


def nn(a, b):
    return lax.dot_general(a, b, (((1,), (0,)), ((), ())), preferred_element_type=F32)


def tn(a, b):
    return lax.dot_general(a, b, (((0,), (0,)), ((), ())), preferred_element_type=F32)


def call(body, ins, outs, flops, nbytes, scratch=(), limit=LIMIT):
    return pl.pallas_call(
        body,
        in_specs=ins,
        out_specs=tuple(VM for _ in outs),
        out_shape=tuple(jax.ShapeDtypeStruct(s, d) for s, d in outs),
        scratch_shapes=list(scratch),
        compiler_params=pltpu.CompilerParams(vmem_limit_bytes=limit),
        cost_estimate=pl.CostEstimate(flops=flops, bytes_accessed=nbytes, transcendentals=0),
    )


def pack_kernel(slot_ref, grad_hbm, saved_hbm, out_ref, square, grad_ref, saved_ref, sems):
    heads, rows = out_ref.shape[0], grad_ref.shape[0]
    half = heads * HD // 2
    copies = []
    for i in range(2):
        part = slice(i * half, (i + 1) * half)
        for j, (src, dst) in enumerate(((grad_hbm, grad_ref), (saved_hbm, saved_ref))):
            copy = pltpu.make_async_copy(src.at[:, part], dst.at[:, part], sems.at[i, j])
            copy.start()
            copies.append(copy)
    square[...] = jnp.zeros_like(square)
    lane = lax.broadcasted_iota(jnp.int32, (rows, BLK), 1)
    delta = jnp.zeros((rows, BLK), F32)
    for h in range(heads):
        if h % (heads // 2) == 0:
            for copy in copies[:2]:
                copy.wait()
            copies = copies[2:]
        g = grad_ref[:, h * HD : (h + 1) * HD]
        for k in range(rows // 2):
            out_ref[h, k] = g[2 * k : 2 * k + 2, :]
        prod = g.astype(F32) * saved_ref[:, h * HD : (h + 1) * HD].astype(F32)
        delta = jnp.where(lane == h, jnp.sum(prod, axis=1, keepdims=True), delta)
    start = pl.multiple_of(slot_ref[0] * rows, rows)
    square[pl.ds(start, rows), :] = delta
    turned = square[...].T
    high = turned.astype(BF16).astype(F32)
    rest = turned - high
    row = lax.broadcasted_iota(jnp.int32, (2, BLK), 0)
    for h in range(heads):
        parts = jnp.where(row == 0, high[h : h + 1, :], rest[h : h + 1, :])
        out_ref[h, rows // 2] = parts.astype(BF16)


def prob_kernel(list_ref, q_ref, k_ref, prev_ref, p_ref):
    span = q_ref.shape[0]
    qcount = span // BLK
    listed = []
    for b in range(qcount):
        bits = jnp.int32(0)
        for slot in range(MAXSEL):
            entry = list_ref[b, slot]
            bits = bits | jnp.where(entry >= 0, jnp.int32(1) << jnp.maximum(entry, 0), 0)
        listed.append(bits)
    lane = lax.broadcasted_iota(jnp.int32, (1, 2 * BLK), 1)
    key_row = lax.broadcasted_iota(jnp.int32, (BLK, 2 * BLK), 0)
    query_col = lax.broadcasted_iota(jnp.int32, (BLK, 2 * BLK), 1)
    for pair in range(qcount // 2):
        first = 2 * pair
        cols = slice(first * BLK, (first + 2) * BLK)
        queries = q_ref[cols, :]
        bits = jnp.where(lane < BLK, listed[first], listed[first + 1])
        keys_of = [(j, prev_ref[j * BLK : (j + 1) * BLK, :]) for j in range(qcount)]
        keys_of += [
            (qcount + j, k_ref[j * BLK : (j + 1) * BLK, :]) for j in range(first + 2)
        ]
        top = jnp.full((BLK, 2 * BLK), MASKED, F32)
        for j, keys in keys_of:
            scores = nt(keys, queries) * SCALE
            allowed = jnp.broadcast_to(((bits >> j) & 1) == 1, scores.shape)
            if j >= qcount + first:
                own = (j - qcount - first) * BLK
                inside = (query_col >= own) & (query_col < own + BLK)
                allowed = allowed & (jnp.logical_not(inside) | (key_row <= query_col - own))
            scores = jnp.where(allowed, scores, MASKED)
            p_ref[j * BLK : (j + 1) * BLK, cols] = scores
            top = jnp.maximum(top, scores)
        top = jnp.max(top, axis=0, keepdims=True)
        total = jnp.zeros((BLK, 2 * BLK), F32)
        for j, _ in keys_of:
            e = jnp.exp(p_ref[j * BLK : (j + 1) * BLK, cols] - top)
            p_ref[j * BLK : (j + 1) * BLK, cols] = e
            total = total + e
        inverse = 1.0 / jnp.sum(total, axis=0, keepdims=True)
        for j, _ in keys_of:
            p_ref[j * BLK : (j + 1) * BLK, cols] = p_ref[j * BLK : (j + 1) * BLK, cols] * inverse
        for j in range(first + 2, qcount):
            rows = slice((qcount + j) * BLK, (qcount + j + 1) * BLK)
            p_ref[rows, cols] = jnp.zeros((BLK, 2 * BLK), F32)


def received(recv_ref):
    peers, pairs = recv_ref.shape[0], recv_ref.shape[1] - 1
    rows = 2 * pairs
    grads = recv_ref[:, 0:pairs].reshape(peers * rows, HD)
    parts = jnp.sum(recv_ref[:, pairs].astype(F32), axis=1)
    each = BLK // rows
    deltas = [
        jnp.sum(parts[b * each : (b + 1) * each], axis=0, keepdims=True)
        for b in range(peers // each)
    ]
    return grads, deltas


def prev_kernel(p_ref, recv_ref, q_ref, prev_ref, back_ref, dq_ref):
    span = q_ref.shape[0]
    grads, deltas = received(recv_ref)
    delta = jnp.concatenate(deltas, axis=1)
    keys, values = prev_ref[0:span, :], prev_ref[span : 2 * span, :]
    p = p_ref[0:span, :]
    score_grad = (p * (nt(values, grads) - delta)).astype(BF16)
    back_ref[0:span, :] = (nn(score_grad, q_ref[...]) * SCALE).astype(BF16)
    back_ref[span : 2 * span, :] = nn(p.astype(BF16), grads).astype(BF16)
    dq_ref[...] = tn(score_grad, keys)


def own_kernel(p_ref, recv_ref, q_ref, k_ref, v_ref, part_ref, dq_ref, dkv_ref):
    span = q_ref.shape[0]
    grads, deltas = received(recv_ref)
    delta = jnp.concatenate(deltas, axis=1)
    p = p_ref[span : 2 * span, :]
    score_grad = (p * (nt(v_ref[...], grads) - delta)).astype(BF16)
    dkv_ref[0:span, :] = nn(score_grad, q_ref[...]) * SCALE
    dkv_ref[span : 2 * span, :] = nn(p.astype(BF16), grads)
    dq_ref[...] = ((part_ref[...] + tn(score_grad, k_ref[...])) * SCALE).astype(BF16)


def join_kernel(dq_ref, dkv_ref, back_ref, out_ref):
    peers, rows = out_ref.shape[0], out_ref.shape[1] // 3
    span = dq_ref.shape[0]
    out_ref[:, 0:rows, :] = dq_ref[...].reshape(peers, rows, HD)
    both = (dkv_ref[...] + back_ref[...].astype(F32)).astype(BF16)
    out_ref[:, rows : 2 * rows, :] = both[0:span].reshape(peers, rows, HD)
    out_ref[:, 2 * rows : 3 * rows, :] = both[span:].reshape(peers, rows, HD)


def split_kernel(in_ref, dq_ref, dk_ref, dv_ref):
    peers, rows = in_ref.shape[0], in_ref.shape[1] // 3
    for h in range(peers):
        for i, ref in enumerate((dq_ref, dk_ref, dv_ref)):
            ref[:, h * HD : (h + 1) * HD] = in_ref[h, i * rows : (i + 1) * rows, :]


def shards(query_heads, key_heads, value_heads, grad_out, saved_out, block_list):
    span = query_heads.shape[0]
    qcount = span // BLK
    heads = lax.axis_size("head")
    rows = grad_out.shape[0]
    slot = lax.rem(lax.axis_index("head"), BLK // rows).astype(jnp.int32)[None]
    (packed,) = call(
        pack_kernel,
        [SM, HB, HB],
        [((heads, rows // 2 + 1, 2, HD), BF16)],
        4 * rows * heads * HD,
        6 * rows * heads * HD,
        [
            pltpu.VMEM((BLK, BLK), F32),
            pltpu.VMEM(grad_out.shape, BF16),
            pltpu.VMEM(saved_out.shape, BF16),
            pltpu.SemaphoreType.DMA((2, 2)),
        ],
        60 * 1024 * 1024,
    )(slot, grad_out, saved_out)
    previous = shifted(jnp.concatenate([key_heads, value_heads], axis=0), "seq", 1)
    arrived = lax.all_to_all(packed, "head", split_axis=0, concat_axis=0, tiled=True)
    group_index = lax.axis_index("seq")
    block_rows = lax.dynamic_slice_in_dim(block_list, group_index * qcount, qcount, 0)
    (probs,) = call(
        prob_kernel,
        [SM, VM, VM, VM],
        [((2 * span, span), F32)],
        4 * span * span * HD,
        12 * span * span,
    )(block_rows, query_heads, key_heads, previous)
    back, dq_part = call(
        prev_kernel,
        [VM] * 4,
        [((2 * span, HD), BF16), ((span, HD), F32)],
        8 * span * span * HD,
        8 * span * span,
    )(probs, arrived, query_heads, previous)
    returned = shifted(back, "seq", -1)
    grad_query, own = call(
        own_kernel,
        [VM] * 6,
        [((span, HD), BF16), ((2 * span, HD), F32)],
        8 * span * span * HD,
        8 * span * span,
    )(probs, arrived, query_heads, key_heads, value_heads, dq_part)
    (joined,) = call(
        join_kernel, [VM] * 3, [((heads, 3 * rows, HD), BF16)], 4 * span * HD, 16 * span * HD
    )(grad_query, own, returned)
    landed = lax.all_to_all(joined, "head", split_axis=0, concat_axis=0, tiled=True)
    return call(
        split_kernel, [VM], [((rows, heads * HD), BF16)] * 3, 0, 12 * rows * heads * HD
    )(landed)


def solution(mesh):
    placed = (
        P("seq", "head"),
        P("seq", "head"),
        P("seq", "head"),
        P(("seq", "head"), None),
        P(("seq", "head"), None),
        P(),
    )
    return jax.shard_map(
        shards,
        mesh=mesh,
        in_specs=placed,
        out_specs=(P(("seq", "head"), None), P(("seq", "head"), None), P(("seq", "head"), None)),
        check_vma=False,
    )
```

```python
import jax
import jax.numpy as jnp
from jax import lax
from jax.experimental import pallas as pl
from jax.experimental.pallas import tpu as pltpu
from jax.sharding import PartitionSpec as P


HD = 128
BLK = 128
MAXSEL = 8
SCALE = HD ** (-0.5)
MASKED = -1e30
LIMIT = 24 * 1024 * 1024
VM = pl.BlockSpec(memory_space=pltpu.VMEM)
SM = pl.BlockSpec(memory_space=pltpu.SMEM)
HB = pl.BlockSpec(memory_space=pltpu.HBM)
F32 = jnp.float32
BF16 = jnp.bfloat16


def shifted(value, axis, by):
    size = lax.axis_size(axis)
    pairs = [(i, i + by) for i in range(size) if 0 <= i + by < size]
    return lax.ppermute(value, axis, pairs)


def turned(value, by):
    size = lax.axis_size("head")
    pairs = [(h, h - h % 8 + (h + 2 * by) % 8) for h in range(size)]
    return lax.ppermute(value, "head", pairs)


def across(value):
    size = lax.axis_size("head")
    groups = [[h for h in range(size) if h % 8 // 2 == z] for z in range(4)]
    return lax.all_to_all(
        value, "head", split_axis=0, concat_axis=0, axis_index_groups=groups, tiled=True
    )


def nt(a, b):
    return lax.dot_general(a, b, (((1,), (1,)), ((), ())), preferred_element_type=F32)


def nn(a, b):
    return lax.dot_general(a, b, (((1,), (0,)), ((), ())), preferred_element_type=F32)


def tn(a, b):
    return lax.dot_general(a, b, (((0,), (0,)), ((), ())), preferred_element_type=F32)


def call(body, ins, outs, flops, nbytes, scratch=(), limit=LIMIT):
    return pl.pallas_call(
        body,
        in_specs=ins,
        out_specs=tuple(VM for _ in outs),
        out_shape=tuple(jax.ShapeDtypeStruct(s, d) for s, d in outs),
        scratch_shapes=list(scratch),
        compiler_params=pltpu.CompilerParams(vmem_limit_bytes=limit),
        cost_estimate=pl.CostEstimate(flops=flops, bytes_accessed=nbytes, transcendentals=0),
    )


def partner(i, z):
    return (i // 2) * 8 + lax.rem(z, 4) * 2 + i % 2


def pack_kernel(
    place_ref, grad_hbm, saved_hbm, k_hbm, v_hbm, *refs
):
    out_refs, (kv_ref, square, grad_ref, saved_ref, sems) = refs[:4], refs[4:]
    rows, heads = grad_ref.shape[0], grad_ref.shape[1] // HD
    span = k_hbm.shape[0]
    copies = []
    for j, (src, dst) in enumerate(
        (
            (grad_hbm, grad_ref),
            (saved_hbm, saved_ref),
            (k_hbm, kv_ref.at[0:span]),
            (v_hbm, kv_ref.at[span : 2 * span]),
        )
    ):
        copy = pltpu.make_async_copy(src, dst, sems.at[j])
        copy.start()
        copies.append(copy)
    square[...] = jnp.zeros_like(square)
    lane = lax.broadcasted_iota(jnp.int32, (rows, BLK), 1)
    delta = jnp.zeros((rows, BLK), F32)
    copies[0].wait()
    copies[1].wait()
    for n in range(heads):
        j, i = n // 8, n % 8
        cols = pl.ds(pl.multiple_of(partner(i, place_ref[1] + j) * HD, HD), HD)
        g = grad_ref[:, cols]
        for k in range(rows // 2):
            out_refs[j][i, k] = g[2 * k : 2 * k + 2, :]
        prod = g.astype(F32) * saved_ref[:, cols].astype(F32)
        delta = jnp.where(lane == n, jnp.sum(prod, axis=1, keepdims=True), delta)
    start = pl.multiple_of(place_ref[0] * rows, rows)
    square[pl.ds(start, rows), :] = delta
    turned = square[...].T
    high = turned.astype(BF16).astype(F32)
    rest = turned - high
    row = lax.broadcasted_iota(jnp.int32, (2, BLK), 0)
    for n in range(heads):
        parts = jnp.where(row == 0, high[n : n + 1, :], rest[n : n + 1, :])
        out_refs[n // 8][n % 8, rows // 2] = parts.astype(BF16)
    copies[2].wait()
    copies[3].wait()


def prob_kernel(list_ref, q_ref, k_ref, prev_ref, p_ref):
    span = q_ref.shape[0]
    qcount = span // BLK
    listed = []
    for b in range(qcount):
        bits = jnp.int32(0)
        for slot in range(MAXSEL):
            entry = list_ref[b, slot]
            bits = bits | jnp.where(entry >= 0, jnp.int32(1) << jnp.maximum(entry, 0), 0)
        listed.append(bits)
    lane = lax.broadcasted_iota(jnp.int32, (1, 2 * BLK), 1)
    key_row = lax.broadcasted_iota(jnp.int32, (BLK, 2 * BLK), 0)
    query_col = lax.broadcasted_iota(jnp.int32, (BLK, 2 * BLK), 1)
    for pair in range(qcount // 2):
        first = 2 * pair
        cols = slice(first * BLK, (first + 2) * BLK)
        queries = q_ref[cols, :]
        bits = jnp.where(lane < BLK, listed[first], listed[first + 1])
        keys_of = [(j, prev_ref[j * BLK : (j + 1) * BLK, :]) for j in range(qcount)]
        keys_of += [
            (qcount + j, k_ref[j * BLK : (j + 1) * BLK, :]) for j in range(first + 2)
        ]
        top = jnp.full((BLK, 2 * BLK), MASKED, F32)
        for j, keys in keys_of:
            scores = nt(keys, queries) * SCALE
            allowed = jnp.broadcast_to(((bits >> j) & 1) == 1, scores.shape)
            if j >= qcount + first:
                own = (j - qcount - first) * BLK
                inside = (query_col >= own) & (query_col < own + BLK)
                allowed = allowed & (jnp.logical_not(inside) | (key_row <= query_col - own))
            scores = jnp.where(allowed, scores, MASKED)
            p_ref[j * BLK : (j + 1) * BLK, cols] = scores
            top = jnp.maximum(top, scores)
        top = jnp.max(top, axis=0, keepdims=True)
        total = jnp.zeros((BLK, 2 * BLK), F32)
        for j, _ in keys_of:
            e = jnp.exp(p_ref[j * BLK : (j + 1) * BLK, cols] - top)
            p_ref[j * BLK : (j + 1) * BLK, cols] = e
            total = total + e
        inverse = 1.0 / jnp.sum(total, axis=0, keepdims=True)
        for j, _ in keys_of:
            p_ref[j * BLK : (j + 1) * BLK, cols] = p_ref[j * BLK : (j + 1) * BLK, cols] * inverse
        for j in range(first + 2, qcount):
            rows = slice((qcount + j) * BLK, (qcount + j + 1) * BLK)
            p_ref[rows, cols] = jnp.zeros((BLK, 2 * BLK), F32)


def prev_kernel(place_ref, p_ref, recv_ref, q_ref, prev_ref, back_ref, dq_ref, grad_ref, delta_ref):
    span = q_ref.shape[0]
    pairs = recv_ref.shape[2] - 1
    rows = 2 * pairs
    for i in range(8):
        for j in range(4):
            start = pl.multiple_of(partner(i, place_ref[1] + 4 - j) * rows, rows)
            grad_ref[pl.ds(start, rows), :] = recv_ref[i, j, 0:pairs].reshape(rows, HD)
    for b in range(span // BLK):
        parts = recv_ref[2 * b : 2 * b + 2, :, pairs].astype(F32)
        delta_ref[:, b * BLK : (b + 1) * BLK] = jnp.sum(
            parts.reshape(16, HD), axis=0, keepdims=True
        )
    grads, delta = grad_ref[...], delta_ref[...]
    keys, values = prev_ref[0:span, :], prev_ref[span : 2 * span, :]
    p = p_ref[0:span, :]
    score_grad = (p * (nt(values, grads) - delta)).astype(BF16)
    back_ref[0:span, :] = (nn(score_grad, q_ref[...]) * SCALE).astype(BF16)
    back_ref[span : 2 * span, :] = nn(p.astype(BF16), grads).astype(BF16)
    dq_ref[...] = tn(score_grad, keys)


def own_kernel(p_ref, grad_ref, delta_ref, q_ref, k_ref, v_ref, part_ref, dq_ref, dkv_ref):
    span = q_ref.shape[0]
    grads, delta = grad_ref[...], delta_ref[...]
    p = p_ref[span : 2 * span, :]
    score_grad = (p * (nt(v_ref[...], grads) - delta)).astype(BF16)
    dkv_ref[0:span, :] = nn(score_grad, q_ref[...]) * SCALE
    dkv_ref[span : 2 * span, :] = nn(p.astype(BF16), grads)
    dq_ref[...] = ((part_ref[...] + tn(score_grad, k_ref[...])) * SCALE).astype(BF16)


def join_kernel(dq_ref, dkv_ref, back_ref, out_ref):
    peers, rows = out_ref.shape[0], out_ref.shape[1] // 3
    span = dq_ref.shape[0]
    out_ref[:, 0:rows, :] = dq_ref[...].reshape(peers, rows, HD)
    both = (dkv_ref[...] + back_ref[...].astype(F32)).astype(BF16)
    out_ref[:, rows : 2 * rows, :] = both[0:span].reshape(peers, rows, HD)
    out_ref[:, 2 * rows : 3 * rows, :] = both[span:].reshape(peers, rows, HD)


def split_kernel(in_ref, dq_ref, dk_ref, dv_ref):
    peers, rows = in_ref.shape[0], in_ref.shape[1] // 3
    for h in range(peers):
        for i, ref in enumerate((dq_ref, dk_ref, dv_ref)):
            ref[:, h * HD : (h + 1) * HD] = in_ref[h, i * rows : (i + 1) * rows, :]


def shards(query_heads, key_heads, value_heads, grad_out, saved_out, block_list):
    span = query_heads.shape[0]
    qcount = span // BLK
    heads = lax.axis_size("head")
    rows = grad_out.shape[0]
    at = lax.axis_index("head").astype(jnp.int32)
    place = jnp.stack([lax.rem(at, 8), lax.rem(at // 2, 4)])
    slab = (8, rows // 2 + 1, 2, HD)
    *slabs, both = call(
        pack_kernel,
        [SM, HB, HB, HB, HB],
        [(slab, BF16)] * 4 + [((2 * span, HD), BF16)],
        4 * rows * heads * HD,
        6 * rows * heads * HD,
        [
            pltpu.VMEM((BLK, BLK), F32),
            pltpu.VMEM(grad_out.shape, BF16),
            pltpu.VMEM(saved_out.shape, BF16),
            pltpu.SemaphoreType.DMA((4,)),
        ],
        60 * 1024 * 1024,
    )(place, grad_out, saved_out, key_heads, value_heads)
    for j in (2, 1, 3):
        slabs[j] = turned(slabs[j], j)
    previous = shifted(both, "seq", 1)
    arrived = across(jnp.stack(slabs, axis=1))
    group_index = lax.axis_index("seq")
    block_rows = lax.dynamic_slice_in_dim(block_list, group_index * qcount, qcount, 0)
    (probs,) = call(
        prob_kernel,
        [SM, VM, VM, VM],
        [((2 * span, span), F32)],
        4 * span * span * HD,
        12 * span * span,
    )(block_rows, query_heads, key_heads, previous)
    back, dq_part, grads, delta = call(
        prev_kernel,
        [SM] + [VM] * 4,
        [((2 * span, HD), BF16), ((span, HD), F32), ((span, HD), BF16), ((1, span), F32)],
        8 * span * span * HD,
        8 * span * span,
    )(place, probs, arrived, query_heads, previous)
    returned = shifted(back, "seq", -1)
    grad_query, own = call(
        own_kernel,
        [VM] * 7,
        [((span, HD), BF16), ((2 * span, HD), F32)],
        8 * span * span * HD,
        8 * span * span,
    )(probs, grads, delta, query_heads, key_heads, value_heads, dq_part)
    (joined,) = call(
        join_kernel, [VM] * 3, [((heads, 3 * rows, HD), BF16)], 4 * span * HD, 16 * span * HD
    )(grad_query, own, returned)
    landed = lax.all_to_all(joined, "head", split_axis=0, concat_axis=0, tiled=True)
    return call(
        split_kernel, [VM], [((rows, heads * HD), BF16)] * 3, 0, 12 * rows * heads * HD
    )(landed)


def solution(mesh):
    placed = (
        P("seq", "head"),
        P("seq", "head"),
        P("seq", "head"),
        P(("seq", "head"), None),
        P(("seq", "head"), None),
        P(),
    )
    return jax.shard_map(
        shards,
        mesh=mesh,
        in_specs=placed,
        out_specs=(P(("seq", "head"), None), P(("seq", "head"), None), P(("seq", "head"), None)),
        check_vma=False,
    )
```

```python
import jax
import jax.numpy as jnp
from jax import lax
from jax.experimental import pallas as pl
from jax.experimental.pallas import tpu as pltpu
from jax.sharding import PartitionSpec as P


HD = 128
BLK = 128
MAXSEL = 8
SCALE = HD ** (-0.5)
MASKED = -1e30
LIMIT = 24 * 1024 * 1024
VM = pl.BlockSpec(memory_space=pltpu.VMEM)
SM = pl.BlockSpec(memory_space=pltpu.SMEM)
HB = pl.BlockSpec(memory_space=pltpu.HBM)
F32 = jnp.float32
BF16 = jnp.bfloat16


def shifted(value, axis, by):
    size = lax.axis_size(axis)
    pairs = [(i, i + by) for i in range(size) if 0 <= i + by < size]
    return lax.ppermute(value, axis, pairs)


def turned(value, by):
    size = lax.axis_size("head")
    pairs = [(h, h - h % 8 + (h + 2 * by) % 8) for h in range(size)]
    return lax.ppermute(value, "head", pairs)


def across(value):
    size = lax.axis_size("head")
    groups = [[h for h in range(size) if h % 8 // 2 == z] for z in range(4)]
    return lax.all_to_all(
        value, "head", split_axis=0, concat_axis=0, axis_index_groups=groups, tiled=True
    )


def nt(a, b):
    return lax.dot_general(a, b, (((1,), (1,)), ((), ())), preferred_element_type=F32)


def nn(a, b):
    return lax.dot_general(a, b, (((1,), (0,)), ((), ())), preferred_element_type=F32)


def tn(a, b):
    return lax.dot_general(a, b, (((0,), (0,)), ((), ())), preferred_element_type=F32)


def call(body, ins, outs, flops, nbytes, scratch=(), limit=LIMIT):
    return pl.pallas_call(
        body,
        in_specs=ins,
        out_specs=tuple(VM for _ in outs),
        out_shape=tuple(jax.ShapeDtypeStruct(s, d) for s, d in outs),
        scratch_shapes=list(scratch),
        compiler_params=pltpu.CompilerParams(vmem_limit_bytes=limit),
        cost_estimate=pl.CostEstimate(flops=flops, bytes_accessed=nbytes, transcendentals=0),
    )


def z_of(place_ref):
    return lax.rem(place_ref[0] // 2, 4)


def partner(i, z):
    return (i // 2) * 8 + lax.rem(z, 4) * 2 + i % 2


def pack_kernel(
    place_ref, grad_hbm, saved_hbm, k_hbm, v_hbm, *refs
):
    out_refs, (kv_ref, square, grad_ref, saved_ref, sems) = refs[:4], refs[4:]
    rows, heads = grad_ref.shape[0], grad_ref.shape[1] // HD
    span = k_hbm.shape[0]
    copies = []
    for j, (src, dst) in enumerate(
        (
            (grad_hbm, grad_ref),
            (saved_hbm, saved_ref),
            (k_hbm, kv_ref.at[0:span]),
            (v_hbm, kv_ref.at[span : 2 * span]),
        )
    ):
        copy = pltpu.make_async_copy(src, dst, sems.at[j])
        copy.start()
        copies.append(copy)
    square[...] = jnp.zeros_like(square)
    lane = lax.broadcasted_iota(jnp.int32, (rows, BLK), 1)
    delta = jnp.zeros((rows, BLK), F32)
    copies[0].wait()
    copies[1].wait()
    for n in range(heads):
        j, i = n // 8, n % 8
        cols = pl.ds(pl.multiple_of(partner(i, z_of(place_ref) + j) * HD, HD), HD)
        g = grad_ref[:, cols]
        for k in range(rows // 2):
            out_refs[j][i, k] = g[2 * k : 2 * k + 2, :]
        prod = g.astype(F32) * saved_ref[:, cols].astype(F32)
        delta = jnp.where(lane == n, jnp.sum(prod, axis=1, keepdims=True), delta)
    start = pl.multiple_of(lax.rem(place_ref[0], 8) * rows, rows)
    square[pl.ds(start, rows), :] = delta
    turned = square[...].T
    high = turned.astype(BF16).astype(F32)
    rest = turned - high
    row = lax.broadcasted_iota(jnp.int32, (2, BLK), 0)
    for n in range(heads):
        parts = jnp.where(row == 0, high[n : n + 1, :], rest[n : n + 1, :])
        out_refs[n // 8][n % 8, rows // 2] = parts.astype(BF16)
    copies[2].wait()
    copies[3].wait()


def prob_kernel(list_ref, q_ref, k_ref, prev_ref, p_ref):
    span = q_ref.shape[0]
    qcount = span // BLK
    listed = []
    for b in range(qcount):
        bits = jnp.int32(0)
        for slot in range(MAXSEL):
            entry = list_ref[b, slot]
            bits = bits | jnp.where(entry >= 0, jnp.int32(1) << jnp.maximum(entry, 0), 0)
        listed.append(bits)
    lane = lax.broadcasted_iota(jnp.int32, (1, 2 * BLK), 1)
    key_row = lax.broadcasted_iota(jnp.int32, (BLK, 2 * BLK), 0)
    query_col = lax.broadcasted_iota(jnp.int32, (BLK, 2 * BLK), 1)
    for pair in range(qcount // 2):
        first = 2 * pair
        cols = slice(first * BLK, (first + 2) * BLK)
        queries = q_ref[cols, :]
        bits = jnp.where(lane < BLK, listed[first], listed[first + 1])
        keys_of = [(j, prev_ref[j * BLK : (j + 1) * BLK, :]) for j in range(qcount)]
        keys_of += [
            (qcount + j, k_ref[j * BLK : (j + 1) * BLK, :]) for j in range(first + 2)
        ]
        top = jnp.full((BLK, 2 * BLK), MASKED, F32)
        for j, keys in keys_of:
            scores = nt(keys, queries) * SCALE
            allowed = jnp.broadcast_to(((bits >> j) & 1) == 1, scores.shape)
            if j >= qcount + first:
                own = (j - qcount - first) * BLK
                inside = (query_col >= own) & (query_col < own + BLK)
                allowed = allowed & (jnp.logical_not(inside) | (key_row <= query_col - own))
            scores = jnp.where(allowed, scores, MASKED)
            p_ref[j * BLK : (j + 1) * BLK, cols] = scores
            top = jnp.maximum(top, scores)
        top = jnp.max(top, axis=0, keepdims=True)
        total = jnp.zeros((BLK, 2 * BLK), F32)
        for j, _ in keys_of:
            e = jnp.exp(p_ref[j * BLK : (j + 1) * BLK, cols] - top)
            p_ref[j * BLK : (j + 1) * BLK, cols] = e
            total = total + e
        inverse = 1.0 / jnp.sum(total, axis=0, keepdims=True)
        for j, _ in keys_of:
            p_ref[j * BLK : (j + 1) * BLK, cols] = p_ref[j * BLK : (j + 1) * BLK, cols] * inverse
        for j in range(first + 2, qcount):
            rows = slice((qcount + j) * BLK, (qcount + j + 1) * BLK)
            p_ref[rows, cols] = jnp.zeros((BLK, 2 * BLK), F32)


def prev_kernel(place_ref, p_ref, recv_ref, q_ref, prev_ref, back_ref, dq_ref, grad_ref, delta_ref):
    span = q_ref.shape[0]
    pairs = recv_ref.shape[2] - 1
    rows = 2 * pairs
    for i in range(8):
        for j in range(4):
            start = pl.multiple_of(partner(i, z_of(place_ref) + 4 - j) * rows, rows)
            grad_ref[pl.ds(start, rows), :] = recv_ref[i, j, 0:pairs].reshape(rows, HD)
    for b in range(span // BLK):
        parts = recv_ref[2 * b : 2 * b + 2, :, pairs].astype(F32)
        delta_ref[:, b * BLK : (b + 1) * BLK] = jnp.sum(
            parts.reshape(16, HD), axis=0, keepdims=True
        )
    grads, delta = grad_ref[...], delta_ref[...]
    keys, values = prev_ref[0:span, :], prev_ref[span : 2 * span, :]
    p = p_ref[0:span, :]
    score_grad = (p * (nt(values, grads) - delta)).astype(BF16)
    back_ref[0:span, :] = (nn(score_grad, q_ref[...]) * SCALE).astype(BF16)
    back_ref[span : 2 * span, :] = nn(p.astype(BF16), grads).astype(BF16)
    dq_ref[...] = tn(score_grad, keys)


def own_kernel(p_ref, grad_ref, delta_ref, q_ref, k_ref, v_ref, part_ref, dq_ref, dkv_ref):
    span = q_ref.shape[0]
    grads, delta = grad_ref[...], delta_ref[...]
    p = p_ref[span : 2 * span, :]
    score_grad = (p * (nt(v_ref[...], grads) - delta)).astype(BF16)
    dkv_ref[0:span, :] = nn(score_grad, q_ref[...]) * SCALE
    dkv_ref[span : 2 * span, :] = nn(p.astype(BF16), grads)
    dq_ref[...] = ((part_ref[...] + tn(score_grad, k_ref[...])) * SCALE).astype(BF16)


def stack_kernel(*refs):
    for j, ref in enumerate(refs[:-1]):
        refs[-1][:, j] = ref[...]


def join_kernel(place_ref, dq_ref, dkv_ref, back_ref, *out_refs):
    rows, span = out_refs[0].shape[1] // 3, dq_ref.shape[0]
    for j in range(4):
        for i in range(8):
            start = partner(i, z_of(place_ref) + j) * rows
            out_refs[j][i, 0:rows, :] = dq_ref[pl.ds(pl.multiple_of(start, rows), rows), :]
            for n in range(2):
                at = pl.ds(pl.multiple_of(start + n * span, rows), rows)
                total = dkv_ref[at, :] + back_ref[at, :].astype(F32)
                out_refs[j][i, (n + 1) * rows : (n + 2) * rows, :] = total.astype(BF16)


def split_kernel(place_ref, *refs):
    in_refs, out_refs = refs[:4], refs[4:]
    peers, rows = in_refs[0].shape[0], in_refs[0].shape[1] // 3
    for j in range(4):
        for i in range(peers):
            start = partner(i, z_of(place_ref) + 4 - j) * HD
            for n, ref in enumerate(out_refs):
                piece = in_refs[j][i, n * rows : (n + 1) * rows, :]
                ref[:, pl.ds(pl.multiple_of(start, HD), HD)] = piece


def shards(query_heads, key_heads, value_heads, grad_out, saved_out, block_list):
    span = query_heads.shape[0]
    qcount = span // BLK
    heads = lax.axis_size("head")
    rows = grad_out.shape[0]
    at = lax.axis_index("head").astype(jnp.int32)
    place = at[None]
    slab = (8, rows // 2 + 1, 2, HD)
    *slabs, both = call(
        pack_kernel,
        [SM, HB, HB, HB, HB],
        [(slab, BF16)] * 4 + [((2 * span, HD), BF16)],
        4 * rows * heads * HD,
        6 * rows * heads * HD,
        [
            pltpu.VMEM((BLK, BLK), F32),
            pltpu.VMEM(grad_out.shape, BF16),
            pltpu.VMEM(saved_out.shape, BF16),
            pltpu.SemaphoreType.DMA((4,)),
        ],
        60 * 1024 * 1024,
    )(place, grad_out, saved_out, key_heads, value_heads)
    for j in (2, 1, 3):
        slabs[j] = turned(slabs[j], j)
    previous = shifted(both, "seq", 1)
    (stacked,) = call(
        stack_kernel, [VM] * 4, [((8, 4) + slab[1:], BF16)], 0, 4 * rows * heads * HD
    )(*slabs)
    arrived = across(stacked)
    group_index = lax.axis_index("seq")
    block_rows = lax.dynamic_slice_in_dim(block_list, group_index * qcount, qcount, 0)
    (probs,) = call(
        prob_kernel,
        [SM, VM, VM, VM],
        [((2 * span, span), F32)],
        4 * span * span * HD,
        12 * span * span,
    )(block_rows, query_heads, key_heads, previous)
    back, dq_part, grads, delta = call(
        prev_kernel,
        [SM] + [VM] * 4,
        [((2 * span, HD), BF16), ((span, HD), F32), ((span, HD), BF16), ((1, span), F32)],
        8 * span * span * HD,
        8 * span * span,
    )(place, probs, arrived, query_heads, previous)
    returned = shifted(back, "seq", -1)
    grad_query, own = call(
        own_kernel,
        [VM] * 7,
        [((span, HD), BF16), ((2 * span, HD), F32)],
        8 * span * span * HD,
        8 * span * span,
    )(probs, grads, delta, query_heads, key_heads, value_heads, dq_part)
    pieces = list(
        call(
            join_kernel,
            [SM] + [VM] * 3,
            [((8, 3 * rows, HD), BF16)] * 4,
            4 * span * HD,
            16 * span * HD,
        )(place, grad_query, own, returned)
    )
    for j in (2, 1, 3):
        pieces[j] = turned(pieces[j], j)
    for j in (0, 1, 3, 2):
        pieces[j] = across(pieces[j])
    return call(
        split_kernel, [SM] + [VM] * 4, [((rows, heads * HD), BF16)] * 3, 0, 12 * rows * heads * HD
    )(place, *pieces)


def solution(mesh):
    placed = (
        P("seq", "head"),
        P("seq", "head"),
        P("seq", "head"),
        P(("seq", "head"), None),
        P(("seq", "head"), None),
        P(),
    )
    return jax.shard_map(
        shards,
        mesh=mesh,
        in_specs=placed,
        out_specs=(P(("seq", "head"), None), P(("seq", "head"), None), P(("seq", "head"), None)),
        check_vma=False,
    )
```

```python
import jax
import jax.numpy as jnp
from jax import lax
from jax.experimental import pallas as pl
from jax.experimental.pallas import tpu as pltpu
from jax.sharding import PartitionSpec as P


HD = 128
BLK = 128
MAXSEL = 8
SCALE = HD ** (-0.5)
MASKED = -1e30
LIMIT = 24 * 1024 * 1024
VM = pl.BlockSpec(memory_space=pltpu.VMEM)
SM = pl.BlockSpec(memory_space=pltpu.SMEM)
HB = pl.BlockSpec(memory_space=pltpu.HBM)
F32 = jnp.float32
BF16 = jnp.bfloat16


def shifted(value, axis, by):
    size = lax.axis_size(axis)
    pairs = [(i, i + by) for i in range(size) if 0 <= i + by < size]
    return lax.ppermute(value, axis, pairs)


def turned(value, by):
    size = lax.axis_size("head")
    pairs = [(h, h - h % 8 + (h + 2 * by) % 8) for h in range(size)]
    return lax.ppermute(value, "head", pairs)


def across(value):
    size = lax.axis_size("head")
    groups = [[h for h in range(size) if h % 8 // 2 == z] for z in range(4)]
    return lax.all_to_all(
        value, "head", split_axis=0, concat_axis=0, axis_index_groups=groups, tiled=True
    )


def nt(a, b):
    return lax.dot_general(a, b, (((1,), (1,)), ((), ())), preferred_element_type=F32)


def nn(a, b):
    return lax.dot_general(a, b, (((1,), (0,)), ((), ())), preferred_element_type=F32)


def tn(a, b):
    return lax.dot_general(a, b, (((0,), (0,)), ((), ())), preferred_element_type=F32)


def call(body, ins, outs, flops, nbytes, scratch=(), limit=LIMIT):
    return pl.pallas_call(
        body,
        in_specs=ins,
        out_specs=tuple(VM for _ in outs),
        out_shape=tuple(jax.ShapeDtypeStruct(s, d) for s, d in outs),
        scratch_shapes=list(scratch),
        compiler_params=pltpu.CompilerParams(vmem_limit_bytes=limit),
        cost_estimate=pl.CostEstimate(flops=flops, bytes_accessed=nbytes, transcendentals=0),
    )


def z_of(place_ref):
    return lax.rem(place_ref[0] // 2, 4)


def partner(i, z):
    return (i // 2) * 8 + lax.rem(z, 4) * 2 + i % 2


def pack_kernel(
    place_ref, grad_hbm, saved_hbm, k_hbm, v_hbm, *refs
):
    out_refs, (kv_ref, square, grad_ref, saved_ref, sems) = refs[:4], refs[4:]
    rows, heads = grad_ref.shape[0], grad_ref.shape[1] // HD
    span = k_hbm.shape[0]
    copies = []
    for j, (src, dst) in enumerate(
        (
            (grad_hbm, grad_ref),
            (saved_hbm, saved_ref),
            (k_hbm, kv_ref.at[0:span]),
            (v_hbm, kv_ref.at[span : 2 * span]),
        )
    ):
        copy = pltpu.make_async_copy(src, dst, sems.at[j])
        copy.start()
        copies.append(copy)
    square[...] = jnp.zeros_like(square)
    lane = lax.broadcasted_iota(jnp.int32, (rows, BLK), 1)
    delta = jnp.zeros((rows, BLK), F32)
    copies[0].wait()
    copies[1].wait()
    for n in range(heads):
        j, i = n // 8, n % 8
        cols = pl.ds(pl.multiple_of(partner(i, z_of(place_ref) + j) * HD, HD), HD)
        g = grad_ref[:, cols]
        for k in range(rows // 2):
            out_refs[j][i, k] = g[2 * k : 2 * k + 2, :]
        prod = g.astype(F32) * saved_ref[:, cols].astype(F32)
        delta = jnp.where(lane == n, jnp.sum(prod, axis=1, keepdims=True), delta)
    start = pl.multiple_of(lax.rem(place_ref[0], 8) * rows, rows)
    square[pl.ds(start, rows), :] = delta
    turned = square[...].T
    high = turned.astype(BF16).astype(F32)
    rest = turned - high
    row = lax.broadcasted_iota(jnp.int32, (2, BLK), 0)
    for n in range(heads):
        parts = jnp.where(row == 0, high[n : n + 1, :], rest[n : n + 1, :])
        out_refs[n // 8][n % 8, rows // 2] = parts.astype(BF16)
    copies[2].wait()
    copies[3].wait()


def prob_kernel(list_ref, q_ref, k_ref, prev_ref, p_ref):
    span = q_ref.shape[0]
    qcount = span // BLK
    listed = []
    for b in range(qcount):
        bits = jnp.int32(0)
        for slot in range(MAXSEL):
            entry = list_ref[b, slot]
            bits = bits | jnp.where(entry >= 0, jnp.int32(1) << jnp.maximum(entry, 0), 0)
        listed.append(bits)
    lane = lax.broadcasted_iota(jnp.int32, (1, 2 * BLK), 1)
    key_row = lax.broadcasted_iota(jnp.int32, (BLK, 2 * BLK), 0)
    query_col = lax.broadcasted_iota(jnp.int32, (BLK, 2 * BLK), 1)
    for pair in range(qcount // 2):
        first = 2 * pair
        cols = slice(first * BLK, (first + 2) * BLK)
        queries = q_ref[cols, :]
        bits = jnp.where(lane < BLK, listed[first], listed[first + 1])
        keys_of = [(j, prev_ref[j * BLK : (j + 1) * BLK, :]) for j in range(qcount)]
        keys_of += [
            (qcount + j, k_ref[j * BLK : (j + 1) * BLK, :]) for j in range(first + 2)
        ]
        top = jnp.full((BLK, 2 * BLK), MASKED, F32)
        for j, keys in keys_of:
            scores = nt(keys, queries) * SCALE
            allowed = jnp.broadcast_to(((bits >> j) & 1) == 1, scores.shape)
            if j >= qcount + first:
                own = (j - qcount - first) * BLK
                inside = (query_col >= own) & (query_col < own + BLK)
                allowed = allowed & (jnp.logical_not(inside) | (key_row <= query_col - own))
            scores = jnp.where(allowed, scores, MASKED)
            p_ref[j * BLK : (j + 1) * BLK, cols] = scores
            top = jnp.maximum(top, scores)
        top = jnp.max(top, axis=0, keepdims=True)
        total = jnp.zeros((BLK, 2 * BLK), F32)
        for j, _ in keys_of:
            e = jnp.exp(p_ref[j * BLK : (j + 1) * BLK, cols] - top)
            p_ref[j * BLK : (j + 1) * BLK, cols] = e
            total = total + e
        inverse = 1.0 / jnp.sum(total, axis=0, keepdims=True)
        for j, _ in keys_of:
            p_ref[j * BLK : (j + 1) * BLK, cols] = p_ref[j * BLK : (j + 1) * BLK, cols] * inverse
        for j in range(first + 2, qcount):
            rows = slice((qcount + j) * BLK, (qcount + j + 1) * BLK)
            p_ref[rows, cols] = jnp.zeros((BLK, 2 * BLK), F32)


def prev_kernel(place_ref, p_ref, recv_ref, q_ref, prev_ref, back_ref, dq_ref, grad_ref, delta_ref):
    span = q_ref.shape[0]
    pairs = recv_ref.shape[2] - 1
    rows = 2 * pairs
    for i in range(8):
        for j in range(4):
            start = pl.multiple_of(partner(i, z_of(place_ref) + 4 - j) * rows, rows)
            grad_ref[pl.ds(start, rows), :] = recv_ref[i, j, 0:pairs].reshape(rows, HD)
    for b in range(span // BLK):
        parts = recv_ref[2 * b : 2 * b + 2, :, pairs].astype(F32)
        delta_ref[:, b * BLK : (b + 1) * BLK] = jnp.sum(
            parts.reshape(16, HD), axis=0, keepdims=True
        )
    grads, delta = grad_ref[...], delta_ref[...]
    keys, values = prev_ref[0:span, :], prev_ref[span : 2 * span, :]
    p = p_ref[0:span, :]
    score_grad = (p * (nt(values, grads) - delta)).astype(BF16)
    back_ref[0:span, :] = (nn(score_grad, q_ref[...]) * SCALE).astype(BF16)
    back_ref[span : 2 * span, :] = nn(p.astype(BF16), grads).astype(BF16)
    dq_ref[...] = tn(score_grad, keys)


def own_kernel(p_ref, grad_ref, delta_ref, q_ref, k_ref, v_ref, part_ref, dq_ref, dkv_ref):
    span = q_ref.shape[0]
    grads, delta = grad_ref[...], delta_ref[...]
    p = p_ref[span : 2 * span, :]
    score_grad = (p * (nt(v_ref[...], grads) - delta)).astype(BF16)
    dkv_ref[0:span, :] = nn(score_grad, q_ref[...]) * SCALE
    dkv_ref[span : 2 * span, :] = nn(p.astype(BF16), grads)
    dq_ref[...] = ((part_ref[...] + tn(score_grad, k_ref[...])) * SCALE).astype(BF16)


def stack_kernel(*refs):
    for j, ref in enumerate(refs[:-1]):
        refs[-1][:, j] = ref[...]


def join_kernel(dq_ref, dkv_ref, back_ref, out_ref):
    peers, rows = out_ref.shape[0], out_ref.shape[1] // 3
    span = dq_ref.shape[0]
    out_ref[:, 0:rows, :] = dq_ref[...].reshape(peers, rows, HD)
    both = (dkv_ref[...] + back_ref[...].astype(F32)).astype(BF16)
    out_ref[:, rows : 2 * rows, :] = both[0:span].reshape(peers, rows, HD)
    out_ref[:, 2 * rows : 3 * rows, :] = both[span:].reshape(peers, rows, HD)


def split_kernel(in_ref, dq_ref, dk_ref, dv_ref):
    peers, rows = in_ref.shape[0], in_ref.shape[1] // 3
    for h in range(peers):
        for i, ref in enumerate((dq_ref, dk_ref, dv_ref)):
            ref[:, h * HD : (h + 1) * HD] = in_ref[h, i * rows : (i + 1) * rows, :]


def shards(query_heads, key_heads, value_heads, grad_out, saved_out, block_list):
    span = query_heads.shape[0]
    qcount = span // BLK
    heads = lax.axis_size("head")
    rows = grad_out.shape[0]
    at = lax.axis_index("head").astype(jnp.int32)
    place = at[None]
    slab = (8, rows // 2 + 1, 2, HD)
    *slabs, both = call(
        pack_kernel,
        [SM, HB, HB, HB, HB],
        [(slab, BF16)] * 4 + [((2 * span, HD), BF16)],
        4 * rows * heads * HD,
        6 * rows * heads * HD,
        [
            pltpu.VMEM((BLK, BLK), F32),
            pltpu.VMEM(grad_out.shape, BF16),
            pltpu.VMEM(saved_out.shape, BF16),
            pltpu.SemaphoreType.DMA((4,)),
        ],
        60 * 1024 * 1024,
    )(place, grad_out, saved_out, key_heads, value_heads)
    for j in (2, 1, 3):
        slabs[j] = turned(slabs[j], j)
    previous = shifted(both, "seq", 1)
    (stacked,) = call(
        stack_kernel, [VM] * 4, [((8, 4) + slab[1:], BF16)], 0, 4 * rows * heads * HD
    )(*slabs)
    arrived = across(stacked)
    group_index = lax.axis_index("seq")
    block_rows = lax.dynamic_slice_in_dim(block_list, group_index * qcount, qcount, 0)
    (probs,) = call(
        prob_kernel,
        [SM, VM, VM, VM],
        [((2 * span, span), F32)],
        4 * span * span * HD,
        12 * span * span,
    )(block_rows, query_heads, key_heads, previous)
    back, dq_part, grads, delta = call(
        prev_kernel,
        [SM] + [VM] * 4,
        [((2 * span, HD), BF16), ((span, HD), F32), ((span, HD), BF16), ((1, span), F32)],
        8 * span * span * HD,
        8 * span * span,
    )(place, probs, arrived, query_heads, previous)
    returned = shifted(back, "seq", -1)
    grad_query, own = call(
        own_kernel,
        [VM] * 7,
        [((span, HD), BF16), ((2 * span, HD), F32)],
        8 * span * span * HD,
        8 * span * span,
    )(probs, grads, delta, query_heads, key_heads, value_heads, dq_part)
    (joined,) = call(
        join_kernel, [VM] * 3, [((heads, 3 * rows, HD), BF16)], 4 * span * HD, 16 * span * HD
    )(grad_query, own, returned)
    landed = lax.all_to_all(joined, "head", split_axis=0, concat_axis=0, tiled=True)
    return call(
        split_kernel, [VM], [((rows, heads * HD), BF16)] * 3, 0, 12 * rows * heads * HD
    )(landed)


def solution(mesh):
    placed = (
        P("seq", "head"),
        P("seq", "head"),
        P("seq", "head"),
        P(("seq", "head"), None),
        P(("seq", "head"), None),
        P(),
    )
    return jax.shard_map(
        shards,
        mesh=mesh,
        in_specs=placed,
        out_specs=(P(("seq", "head"), None), P(("seq", "head"), None), P(("seq", "head"), None)),
        check_vma=False,
    )
```

```python
import jax
import jax.numpy as jnp
from jax import lax
from jax.experimental import pallas as pl
from jax.experimental.pallas import tpu as pltpu
from jax.sharding import PartitionSpec as P


HD = 128
BLK = 128
MAXSEL = 8
SCALE = HD ** (-0.5)
MASKED = -1e30
LIMIT = 24 * 1024 * 1024
VM = pl.BlockSpec(memory_space=pltpu.VMEM)
SM = pl.BlockSpec(memory_space=pltpu.SMEM)
HB = pl.BlockSpec(memory_space=pltpu.HBM)
F32 = jnp.float32
BF16 = jnp.bfloat16


def shifted(value, axis, by):
    size = lax.axis_size(axis)
    pairs = [(i, i + by) for i in range(size) if 0 <= i + by < size]
    return lax.ppermute(value, axis, pairs)


def turned(value, by):
    size = lax.axis_size("head")
    pairs = [(h, h - h % 8 + (h + 2 * by) % 8) for h in range(size)]
    return lax.ppermute(value, "head", pairs)


def across(value):
    size = lax.axis_size("head")
    groups = [[h for h in range(size) if h % 8 // 2 == z] for z in range(4)]
    return lax.all_to_all(
        value, "head", split_axis=0, concat_axis=0, axis_index_groups=groups, tiled=True
    )


def nt(a, b):
    return lax.dot_general(a, b, (((1,), (1,)), ((), ())), preferred_element_type=F32)


def nn(a, b):
    return lax.dot_general(a, b, (((1,), (0,)), ((), ())), preferred_element_type=F32)


def tn(a, b):
    return lax.dot_general(a, b, (((0,), (0,)), ((), ())), preferred_element_type=F32)


def call(body, ins, outs, flops, nbytes, scratch=(), limit=LIMIT):
    return pl.pallas_call(
        body,
        in_specs=ins,
        out_specs=tuple(VM for _ in outs),
        out_shape=tuple(jax.ShapeDtypeStruct(s, d) for s, d in outs),
        scratch_shapes=list(scratch),
        compiler_params=pltpu.CompilerParams(vmem_limit_bytes=limit),
        cost_estimate=pl.CostEstimate(flops=flops, bytes_accessed=nbytes, transcendentals=0),
    )


def z_of(place_ref):
    return lax.rem(place_ref[0] // 2, 4)


def partner(i, z):
    return (i // 2) * 8 + lax.rem(z, 4) * 2 + i % 2


def pack_kernel(place_ref, grad_hbm, saved_hbm, *refs):
    out_refs, (square, grad_ref, saved_ref, sems) = refs[:4], refs[4:]
    rows, heads = grad_ref.shape[0], grad_ref.shape[1] // HD
    copies = []
    for j, (src, dst) in enumerate(((grad_hbm, grad_ref), (saved_hbm, saved_ref))):
        copy = pltpu.make_async_copy(src, dst, sems.at[j])
        copy.start()
        copies.append(copy)
    square[...] = jnp.zeros_like(square)
    lane = lax.broadcasted_iota(jnp.int32, (rows, BLK), 1)
    delta = jnp.zeros((rows, BLK), F32)
    copies[0].wait()
    copies[1].wait()
    for n in range(heads):
        j, i = n // 8, n % 8
        cols = pl.ds(pl.multiple_of(partner(i, z_of(place_ref) + j) * HD, HD), HD)
        g = grad_ref[:, cols]
        for k in range(rows // 2):
            out_refs[j][i, k] = g[2 * k : 2 * k + 2, :]
        prod = g.astype(F32) * saved_ref[:, cols].astype(F32)
        delta = jnp.where(lane == n, jnp.sum(prod, axis=1, keepdims=True), delta)
    start = pl.multiple_of(lax.rem(place_ref[0], 8) * rows, rows)
    square[pl.ds(start, rows), :] = delta
    turned = square[...].T
    high = turned.astype(BF16).astype(F32)
    rest = turned - high
    row = lax.broadcasted_iota(jnp.int32, (2, BLK), 0)
    for n in range(heads):
        parts = jnp.where(row == 0, high[n : n + 1, :], rest[n : n + 1, :])
        out_refs[n // 8][n % 8, rows // 2] = parts.astype(BF16)


def prob_kernel(list_ref, q_ref, k_ref, prev_ref, p_ref):
    span = q_ref.shape[0]
    qcount = span // BLK
    listed = []
    for b in range(qcount):
        bits = jnp.int32(0)
        for slot in range(MAXSEL):
            entry = list_ref[b, slot]
            bits = bits | jnp.where(entry >= 0, jnp.int32(1) << jnp.maximum(entry, 0), 0)
        listed.append(bits)
    lane = lax.broadcasted_iota(jnp.int32, (1, 2 * BLK), 1)
    key_row = lax.broadcasted_iota(jnp.int32, (BLK, 2 * BLK), 0)
    query_col = lax.broadcasted_iota(jnp.int32, (BLK, 2 * BLK), 1)
    for pair in range(qcount // 2):
        first = 2 * pair
        cols = slice(first * BLK, (first + 2) * BLK)
        queries = q_ref[cols, :]
        bits = jnp.where(lane < BLK, listed[first], listed[first + 1])
        keys_of = [(j, prev_ref[j * BLK : (j + 1) * BLK, :]) for j in range(qcount)]
        keys_of += [
            (qcount + j, k_ref[j * BLK : (j + 1) * BLK, :]) for j in range(first + 2)
        ]
        top = jnp.full((BLK, 2 * BLK), MASKED, F32)
        for j, keys in keys_of:
            scores = nt(keys, queries) * SCALE
            allowed = jnp.broadcast_to(((bits >> j) & 1) == 1, scores.shape)
            if j >= qcount + first:
                own = (j - qcount - first) * BLK
                inside = (query_col >= own) & (query_col < own + BLK)
                allowed = allowed & (jnp.logical_not(inside) | (key_row <= query_col - own))
            scores = jnp.where(allowed, scores, MASKED)
            p_ref[j * BLK : (j + 1) * BLK, cols] = scores
            top = jnp.maximum(top, scores)
        top = jnp.max(top, axis=0, keepdims=True)
        total = jnp.zeros((BLK, 2 * BLK), F32)
        for j, _ in keys_of:
            e = jnp.exp(p_ref[j * BLK : (j + 1) * BLK, cols] - top)
            p_ref[j * BLK : (j + 1) * BLK, cols] = e
            total = total + e
        inverse = 1.0 / jnp.sum(total, axis=0, keepdims=True)
        for j, _ in keys_of:
            p_ref[j * BLK : (j + 1) * BLK, cols] = p_ref[j * BLK : (j + 1) * BLK, cols] * inverse
        for j in range(first + 2, qcount):
            rows = slice((qcount + j) * BLK, (qcount + j + 1) * BLK)
            p_ref[rows, cols] = jnp.zeros((BLK, 2 * BLK), F32)


def prev_kernel(
    place_ref, p_ref, recv_ref, q_ref, k_ref, v_ref, back_ref, dq_ref, grad_ref, delta_ref
):
    span = q_ref.shape[0]
    pairs = recv_ref.shape[2] - 1
    rows = 2 * pairs
    for i in range(8):
        for j in range(4):
            start = pl.multiple_of(partner(i, z_of(place_ref) + 4 - j) * rows, rows)
            grad_ref[pl.ds(start, rows), :] = recv_ref[i, j, 0:pairs].reshape(rows, HD)
    for b in range(span // BLK):
        parts = recv_ref[2 * b : 2 * b + 2, :, pairs].astype(F32)
        delta_ref[:, b * BLK : (b + 1) * BLK] = jnp.sum(
            parts.reshape(16, HD), axis=0, keepdims=True
        )
    grads, delta = grad_ref[...], delta_ref[...]
    keys, values = k_ref[...], v_ref[...]
    p = p_ref[0:span, :]
    score_grad = (p * (nt(values, grads) - delta)).astype(BF16)
    back_ref[0:span, :] = (nn(score_grad, q_ref[...]) * SCALE).astype(BF16)
    back_ref[span : 2 * span, :] = nn(p.astype(BF16), grads).astype(BF16)
    dq_ref[...] = tn(score_grad, keys)


def own_kernel(p_ref, grad_ref, delta_ref, q_ref, k_ref, v_ref, part_ref, dq_ref, dkv_ref):
    span = q_ref.shape[0]
    grads, delta = grad_ref[...], delta_ref[...]
    p = p_ref[span : 2 * span, :]
    score_grad = (p * (nt(v_ref[...], grads) - delta)).astype(BF16)
    dkv_ref[0:span, :] = nn(score_grad, q_ref[...]) * SCALE
    dkv_ref[span : 2 * span, :] = nn(p.astype(BF16), grads)
    dq_ref[...] = ((part_ref[...] + tn(score_grad, k_ref[...])) * SCALE).astype(BF16)


def stack_kernel(*refs):
    for j, ref in enumerate(refs[:-1]):
        refs[-1][:, j] = ref[...]


def join_kernel(dq_ref, dkv_ref, back_ref, out_ref):
    peers, rows = out_ref.shape[0], out_ref.shape[1] // 3
    span = dq_ref.shape[0]
    out_ref[:, 0:rows, :] = dq_ref[...].reshape(peers, rows, HD)
    both = (dkv_ref[...] + back_ref[...].astype(F32)).astype(BF16)
    out_ref[:, rows : 2 * rows, :] = both[0:span].reshape(peers, rows, HD)
    out_ref[:, 2 * rows : 3 * rows, :] = both[span:].reshape(peers, rows, HD)


def split_kernel(in_ref, dq_ref, dk_ref, dv_ref):
    peers, rows = in_ref.shape[0], in_ref.shape[1] // 3
    for h in range(peers):
        for i, ref in enumerate((dq_ref, dk_ref, dv_ref)):
            ref[:, h * HD : (h + 1) * HD] = in_ref[h, i * rows : (i + 1) * rows, :]


def shards(query_heads, key_heads, value_heads, grad_out, saved_out, block_list):
    span = query_heads.shape[0]
    qcount = span // BLK
    heads = lax.axis_size("head")
    rows = grad_out.shape[0]
    at = lax.axis_index("head").astype(jnp.int32)
    place = at[None]
    slab = (8, rows // 2 + 1, 2, HD)
    slabs = list(
        call(
            pack_kernel,
            [SM, HB, HB],
            [(slab, BF16)] * 4,
            4 * rows * heads * HD,
            6 * rows * heads * HD,
            [
                pltpu.VMEM((BLK, BLK), F32),
                pltpu.VMEM(grad_out.shape, BF16),
                pltpu.VMEM(saved_out.shape, BF16),
                pltpu.SemaphoreType.DMA((2,)),
            ],
            60 * 1024 * 1024,
        )(place, grad_out, saved_out)
    )
    for j in (2, 1, 3):
        slabs[j] = turned(slabs[j], j)
    prev_keys = shifted(key_heads, "seq", 1)
    prev_values = shifted(value_heads, "seq", 1)
    (stacked,) = call(
        stack_kernel, [VM] * 4, [((8, 4) + slab[1:], BF16)], 0, 4 * rows * heads * HD
    )(*slabs)
    arrived = across(stacked)
    group_index = lax.axis_index("seq")
    block_rows = lax.dynamic_slice_in_dim(block_list, group_index * qcount, qcount, 0)
    (probs,) = call(
        prob_kernel,
        [SM, VM, VM, VM],
        [((2 * span, span), F32)],
        4 * span * span * HD,
        12 * span * span,
    )(block_rows, query_heads, key_heads, prev_keys)
    back, dq_part, grads, delta = call(
        prev_kernel,
        [SM] + [VM] * 5,
        [((2 * span, HD), BF16), ((span, HD), F32), ((span, HD), BF16), ((1, span), F32)],
        8 * span * span * HD,
        8 * span * span,
    )(place, probs, arrived, query_heads, prev_keys, prev_values)
    returned = shifted(back, "seq", -1)
    grad_query, own = call(
        own_kernel,
        [VM] * 7,
        [((span, HD), BF16), ((2 * span, HD), F32)],
        8 * span * span * HD,
        8 * span * span,
    )(probs, grads, delta, query_heads, key_heads, value_heads, dq_part)
    (joined,) = call(
        join_kernel, [VM] * 3, [((heads, 3 * rows, HD), BF16)], 4 * span * HD, 16 * span * HD
    )(grad_query, own, returned)
    landed = lax.all_to_all(joined, "head", split_axis=0, concat_axis=0, tiled=True)
    return call(
        split_kernel, [VM], [((rows, heads * HD), BF16)] * 3, 0, 12 * rows * heads * HD
    )(landed)


def solution(mesh):
    placed = (
        P("seq", "head"),
        P("seq", "head"),
        P("seq", "head"),
        P(("seq", "head"), None),
        P(("seq", "head"), None),
        P(),
    )
    return jax.shard_map(
        shards,
        mesh=mesh,
        in_specs=placed,
        out_specs=(P(("seq", "head"), None), P(("seq", "head"), None), P(("seq", "head"), None)),
        check_vma=False,
    )
```
